128 devices in a mesh: group: 8 (over z, core), tensor: 16 (over y, x).
Axes of the slice: x: 4, y: 4, z: 4, core: 2. Of those that a mesh axis runs over, the one named last changes fastest.
Arguments:
- hidden_rows: bfloat16 [3072, 8192], P('group', 'tensor'), may hold values from -6 to 6
- attn_rows: bfloat16 [3072, 8192], P('group', 'tensor'), may hold values from -6 to 6
- q_weight: bfloat16 [8192, 8192], P(None, 'tensor'), may hold values from -0.0625 to 0.0625
- o_weight: bfloat16 [8192, 8192], P('tensor'), may hold values from -0.0625 to 0.0625
- owner_table: int32 [64], replicated, may hold values from 0 to 63, as said below
- group_adapters: int32 [8, 8], replicated, may hold values from 0 to 63, as said below
- req_slot: int32 [8, 16], P('group'), may hold values from 0 to 7
- req_len: int32 [8, 16], P('group'), may hold values from 1 to 96, 384 in all within a row
- qa_store: bfloat16 [64, 8192, 64], P('group', 'tensor'), may hold values from -0.0625 to 0.0625
- qb_store: bfloat16 [64, 64, 8192], P('group', None, 'tensor'), may hold values from -0.75 to 0.75
- oa_store: bfloat16 [64, 8192, 64], P('group', 'tensor'), may hold values from -0.0625 to 0.0625
- ob_store: bfloat16 [64, 64, 8192], P('group', None, 'tensor'), may hold values from -0.75 to 0.75
Outputs:
- queries: bfloat16 [3072, 8192], P('group', 'tensor')
- attn_out: bfloat16 [3072, 8192], P('group')
The draws below stay inside these ranges and needn't reach their ends.
Inputs may be any that keep to these rules, and one draw needn't show every extreme that they name: A permutation: adapter a sits at storage index owner_table[a], held by index owner_table[a] // 8 of group. `group_adapters`: each row names 8 distinct adapters, exactly 1 of them held by each index of group; different groups may name the same adapter.
All inputs are finite; a program needn't handle non-finite values.
Results may differ from the reference program's by a relative error of at most 0.001.
Values may be sent and summed in bfloat16 or wider, within the bound.
A program may use at most 128 MiB of HBM per device.

```python
import math
import jax
import jax.numpy as jnp
import numpy as np
from jax import lax

D = 8192
R = 64
SLOTS = 8
REQS = 16
ROWS = 384
ADP_DEV = 8
GROUPS = 8
ADAPTERS = 64
MOST = 96
ROWS_ALL = 3072


def layout(key):
    base_product = jax.random.fold_in(key, 11)
    key_table, key_order, key_local = jax.random.split(base_product, 3)
    table = jax.random.permutation(key_table, ADAPTERS).astype(jnp.int32)
    holder = jnp.argsort(table).astype(jnp.int32)
    slot_start_offset = jnp.arange(SLOTS, dtype=jnp.int32)
    owners = slot_start_offset % GROUPS
    member_rank = slot_start_offset // GROUPS

    def local_draw(subkey):
        return jax.random.permutation(subkey, ADP_DEV).astype(jnp.int32)

    def order_draw(subkey):
        return jax.random.permutation(subkey, SLOTS).astype(jnp.int32)
    local_perm = jax.vmap(local_draw)(jax.random.split(key_local, GROUPS))
    chosen = jnp.take(local_perm, member_rank, axis=1)
    storage = owners[None, :] * ADP_DEV + chosen
    orders = jax.vmap(order_draw)(jax.random.split(key_order, GROUPS))
    storage = jnp.take_along_axis(storage, orders, axis=1)
    return (table, jnp.take(holder, storage, axis=0).astype(jnp.int32))


def draw_owner_table(key, part):
    return layout(key)[0]


def draw_group_adapters(key, part):
    return layout(key)[1]


def set_ends(drawn, rng, least, top_value):
    dims = drawn.shape
    spot = [jax.random.randint(jax.random.fold_in(rng, axis), (), 0, dims[axis]) for axis in range(len(dims))]
    drawn = drawn.at[tuple(spot)].set(least)
    longest = dims.index(max(dims))
    spot[longest] = (spot[longest] + 1) % dims[longest]
    return drawn.at[tuple(spot)].set(top_value)


def levels(own_key, extent, shards, least, top_value):
    def one(dim, parts):
        draws = jax.random.uniform(jax.random.fold_in(jax.random.fold_in(own_key, 6), dim), (parts,), jnp.float32, least / len(shards), top_value / len(shards))
        return jnp.repeat(jnp.exp(draws), extent[dim] // parts).reshape((-1,) + (1,) * (len(extent) - dim - 1))

    gain = one(*shards[0])
    for cut in shards[1:]:
        gain = gain * one(*cut)
    return gain


def cumulative_ranks(number_of, slope):
    loads = [(1 << 20) // math.isqrt(rank ** slope) + 1 for rank in range(1, number_of + 1)]
    deviation = 1 + sum(loads) // (1 << 30)
    return np.cumsum(np.array([max(1, weight // deviation) for weight in loads]))


def ranked(rng, extent, count, skew):
    grid = cumulative_ranks(count, skew)
    pick = jax.random.randint(jax.random.fold_in(rng, 1), extent, 0, int(grid[count - 1]))
    standing = jnp.searchsorted(jnp.asarray(grid, jnp.int32), pick, side="right")
    return jax.random.permutation(jax.random.fold_in(rng, 2), count)[standing].astype(jnp.int32)


def profile(count, total, limit, skew):
    weights = [(1 << 20) // math.isqrt(standing ** skew) + 1 for standing in range(2, count + 1)]
    surplus, given = total - limit - (count - 1), [1] * (count - 1)
    while surplus > 0:
        candidates = [i for i in range(count - 1) if given[i] < limit]
        whole, budget = sum([weights[i] for i in candidates]), surplus
        for i in candidates:
            more = min(limit - given[i], max(1, budget * weights[i] // whole), surplus)
            given[i] = given[i] + more
            surplus = surplus - more
    return np.array([limit] + given)


def uneven(own_key, count, total, most, skew):
    if count == 2:
        one = jax.random.randint(own_key, (), max(1, total - most), min(most, total - 1) + 1)
        return jnp.stack([one, total - one])
    tallies = jnp.asarray(profile(count, total, most, skew), jnp.int32)
    pairs = (count - 1) // 2
    donor, taker = tallies[1:1 + 2 * pairs:2], tallies[2:2 + 2 * pairs:2]
    margin = jnp.minimum(donor - 1, most - taker)
    shifted = jax.random.randint(jax.random.fold_in(own_key, 1), (pairs,), 0, 1 << 20) % (margin + 1)
    tallies = tallies.at[1:1 + 2 * pairs:2].set(donor - shifted).at[2:2 + 2 * pairs:2].set(taker + shifted)
    return tallies[jax.random.permutation(jax.random.fold_in(own_key, 2), count)]


def normal_values(rng, dims, scale, limit, cuts=(), held_as=jnp.bfloat16):
    level = levels(rng, dims, cuts, -0.22, 0.18) if cuts else 1.0
    drawn = jax.random.normal(rng, dims, jnp.float32) * scale * level
    return jnp.minimum(jnp.maximum(drawn, -limit), limit).astype(held_as)


def setup_inputs(seed: int = 0) -> dict:
    arg_keys = jax.random.split(jax.random.key(seed), 13)
    hidden_rows = normal_values(arg_keys[0], (ROWS_ALL, D), 1.0, 6.0, ((0, 8), (1, 16)))
    attn_rows = normal_values(arg_keys[1], (ROWS_ALL, D), 1.0, 6.0, ((0, 8), (1, 16)))
    q_weight = normal_values(arg_keys[2], (D, D), D ** -0.5, 0.0625, ((1, 16),))
    o_weight = normal_values(arg_keys[3], (D, D), D ** -0.5, 0.0625, ((0, 16),))
    owner_table = draw_owner_table(jax.random.fold_in(arg_keys[12], 71), 0)
    group_adapters = draw_group_adapters(jax.random.fold_in(arg_keys[12], 71), 0)
    req_slot = set_ends(ranked(arg_keys[6], (GROUPS, REQS), SLOTS, 2), jax.random.fold_in(arg_keys[6], 3), 0, SLOTS - 1).astype(jnp.int32)
    req_len = jax.vmap(lambda own: uneven(own, REQS, ROWS, MOST, 2))(jax.random.split(arg_keys[7], GROUPS)).reshape((GROUPS, REQS)).astype(jnp.int32)
    qa_store = normal_values(arg_keys[8], (ADAPTERS, D, R), D ** -0.5, 0.0625, ((0, 8), (1, 16)))
    qb_store = normal_values(arg_keys[9], (ADAPTERS, R, D), R ** -0.5, 0.75, ((0, 8), (2, 16)))
    oa_store = normal_values(arg_keys[10], (ADAPTERS, D, R), D ** -0.5, 0.0625, ((0, 8), (1, 16)))
    ob_store = normal_values(arg_keys[11], (ADAPTERS, R, D), R ** -0.5, 0.75, ((0, 8), (2, 16)))
    return {"hidden_rows": hidden_rows, "attn_rows": attn_rows, "q_weight": q_weight, "o_weight": o_weight, "owner_table": owner_table, "group_adapters": group_adapters, "req_slot": req_slot, "req_len": req_len, "qa_store": qa_store, "qb_store": qb_store, "oa_store": oa_store, "ob_store": ob_store}


ADAPTER_SCALE = 0.5


def slot_onehot(lengths, slot_ids):
    req_ends = jnp.cumsum(lengths).astype(jnp.int32)
    req_starts = (req_ends - lengths).astype(jnp.int32)
    position = jnp.arange(ROWS, dtype=jnp.int32)[:, None]
    inside = ((position >= req_starts[None, :]) & (position < req_ends[None, :])).astype(jnp.int32)
    slot_row = jnp.sum(inside * slot_ids[None, :], axis=1).astype(jnp.int32)
    return slot_row[:, None] == jnp.arange(SLOTS, dtype=jnp.int32)[None, :]


def adapted(rows_in, weight, down_all, up_all, onehot):
    down_flat = jnp.transpose(down_all, (1, 0, 2)).reshape(down_all.shape[1], SLOTS * R)
    up_weight_flat = up_all.reshape(SLOTS * R, up_all.shape[2]).astype(jnp.float32)
    partial_down = jnp.dot(rows_in, down_flat, preferred_element_type=jnp.float32).reshape(ROWS, SLOTS, R)
    chosen = jnp.sum(onehot.astype(jnp.float32)[:, :, None] * partial_down, axis=1)
    expanded_rows = (onehot.astype(jnp.float32)[:, :, None] * chosen[:, None, :]).reshape(ROWS, SLOTS * R)
    base_product = jnp.dot(rows_in, weight, preferred_element_type=jnp.float32)
    up_term = jnp.dot(expanded_rows, up_weight_flat, precision=lax.Precision.HIGHEST, preferred_element_type=jnp.float32)
    return (base_product + ADAPTER_SCALE * up_term).astype(jnp.bfloat16)


def reference(hidden_rows, attn_rows, q_weight, o_weight, owner_table, group_adapters, req_slot, req_len, qa_store, qb_store, oa_store, ob_store):
    query_parts = []
    output_parts = []
    for group_id in range(GROUPS):
        storage = jnp.take(owner_table, group_adapters[group_id], axis=0).astype(jnp.int32)
        onehot = slot_onehot(req_len[group_id], req_slot[group_id])
        hidden_block = hidden_rows[group_id * ROWS:(group_id + 1) * ROWS]
        attn_block = attn_rows[group_id * ROWS:(group_id + 1) * ROWS]
        query_parts.append(adapted(hidden_block, q_weight, jnp.take(qa_store, storage, axis=0), jnp.take(qb_store, storage, axis=0), onehot))
        output_parts.append(adapted(attn_block, o_weight, jnp.take(oa_store, storage, axis=0), jnp.take(ob_store, storage, axis=0), onehot))
    return jnp.concatenate(query_parts, axis=0), jnp.concatenate(output_parts, axis=0)
```

```python
import jax
import jax.numpy as jnp
from jax import lax
from jax.experimental import pallas as pl
from jax.experimental.pallas import tpu as pltpu
from jax.sharding import PartitionSpec as P

MESH = pl.DeviceIdType.MESH
F32 = jnp.float32
BF16 = jnp.bfloat16

W_Y = 0
W_Z = 6
W_SIB = 18
ATT = 30
ADP_A = 34
ADP_B = 42
DOWN_1 = 50
DOWN_2 = 53
DOWN_3 = 56
RED = 59
HID = 65
OUT = 105
N_SEMS = 145
N_LOCAL = 12


def mod(a, n):
    return lax.rem(a + n, n)


def kernel(
    hidden, attn, q_weight, o_weight, qa, qb, oa, ob, table, adapters, req_slot, req_len,
    q_out, a_out,
    hid_all, attn_all, w_o, w_stage, w_q, qa_v, qb_v, oa_v, ob_v, send_a, send_b, recv_a, recv_b,
    owner_v, down_v, down_1, down_2, down_s, down_all, up_q, up_o, part, r_opp, r_nbr, o_blk, q_blk,
    send_sem, recv_sem, local_sem,
):
    g = lax.axis_index("group")
    t = lax.axis_index("tensor")
    z, c = lax.div(g, 2), lax.rem(g, 2)
    y, x = lax.div(t, 4), lax.rem(t, 4)
    ys = [y, mod(y - 1, 4), mod(y + 1, 4), mod(y + 2, 4)]
    xs = [x, mod(x - 1, 4), mod(x + 1, 4), mod(x + 2, 4)]
    gs = [g] + [mod(z + d, 4) * 2 + c for d in (-1, 1, 2)]
    sib = z * 2 + (1 - c)
    gsib = [sib] + [mod(z + d, 4) * 2 + (1 - c) for d in (-1, 1, 2)]
    dev_x = [None] + [{"tensor": y * 4 + xs[i]} for i in (1, 2, 3)]
    dev_y = [None] + [{"tensor": ys[i] * 4 + x} for i in (1, 2, 3)]
    dev_z = [None] + [{"group": gs[i]} for i in (1, 2)]
    dev_sib = {"group": sib}

    sent = []

    def send(k, src, dst, dev):
        copy = pltpu.make_async_remote_copy(
            src_ref=src, dst_ref=dst, send_sem=send_sem.at[k], recv_sem=recv_sem.at[k],
            device_id=dev, device_id_type=MESH,
        )
        copy.start()
        sent.append(copy)

    def got(k, ref):
        pltpu.make_async_remote_copy(
            src_ref=ref, dst_ref=ref, send_sem=send_sem.at[k], recv_sem=recv_sem.at[k],
            device_id=dev_sib, device_id_type=MESH,
        ).wait_recv()

    def load(k, src, dst):
        copy = pltpu.make_async_copy(src, dst, local_sem.at[k])
        copy.start()
        return copy

    barrier = pltpu.get_barrier_semaphore()
    for i in (1, 2, 3):
        pl.semaphore_signal(barrier, inc=1, device_id=dev_x[i], device_id_type=MESH)
        pl.semaphore_signal(barrier, inc=1, device_id=dev_y[i], device_id_type=MESH)
    for d in range(1, 8):
        pl.semaphore_signal(barrier, inc=1, device_id={"group": mod(g + d, 8)}, device_id_type=MESH)
    col_y = [pl.multiple_of(v * 2048, 2048) for v in ys]
    l_qa, l_oa = load(0, qa, qa_v), load(1, oa, oa_v)
    l_qb, l_ob = load(2, qb, qb_v), load(3, ob, ob_v)
    l_attn = load(4, attn, attn_all.at[y])
    l_hid = load(5, hidden, hid_all.at[t])
    l_wo = load(6, o_weight.at[:, pl.ds(col_y[0], 2048)], w_o.at[y])
    l_wq = load(7, q_weight, w_q)
    pl.semaphore_wait(barrier, 13)

    class Gather:
        def __init__(self, base, buf, own):
            self.base, self.buf, self.own = base, buf, own

        def block(self, half, i, j):
            return ys[j] * 4 + xs[i] if half == 0 else ys[i] * 4 + xs[j]

        def devs(self, half):
            return (dev_x, dev_y) if half == 0 else (dev_y, dev_x)

        def rows(self, half, i, j, quarter=None):
            b = self.block(half, i, j)
            if quarter is None:
                return self.buf.at[b, pl.ds(half * 192, 192)]
            return self.buf.at[b, pl.ds(half * 192 + quarter * 96, 96)]

        def src_own(self, half):
            return self.own.at[pl.ds(half * 192, 192)]

        def first_own(self, half):
            dev = self.devs(half)[0]
            k = self.base + half * 20
            send(k, self.src_own(half), self.rows(half, 0, 0), dev[2])
            send(k + 1, self.src_own(half), self.rows(half, 0, 0), dev[1])

        def first_fwd(self, half):
            dev = self.devs(half)[0]
            k = self.base + half * 20
            got(k, self.rows(half, 1, 0))
            send(k + 2, self.rows(half, 1, 0, 0), self.rows(half, 1, 0, 0), dev[2])
            got(k + 1, self.rows(half, 2, 0))
            send(k + 3, self.rows(half, 2, 0, 1), self.rows(half, 2, 0, 1), dev[1])

        def first_opp(self, half):
            k = self.base + half * 20
            got(k + 2, self.rows(half, 3, 0, 0))
            got(k + 3, self.rows(half, 3, 0, 1))

        def second_own(self, half, i):
            dev = self.devs(half)[1]
            k = self.base + half * 20 + 4 + 4 * i
            src = self.src_own(half) if i == 0 else self.rows(half, i, 0)
            send(k, src, self.rows(half, i, 0), dev[2])
            send(k + 1, src, self.rows(half, i, 0), dev[1])

        def second_fwd(self, half, i):
            dev = self.devs(half)[1]
            k = self.base + half * 20 + 4 + 4 * i
            got(k, self.rows(half, i, 1))
            send(k + 2, self.rows(half, i, 1, 0), self.rows(half, i, 1, 0), dev[2])
            got(k + 1, self.rows(half, i, 2))
            send(k + 3, self.rows(half, i, 2, 1), self.rows(half, i, 2, 1), dev[1])

        def second_opp(self, half, i):
            k = self.base + half * 20 + 4 + 4 * i
            got(k + 2, self.rows(half, i, 3, 0))
            got(k + 3, self.rows(half, i, 3, 1))

    hid = Gather(HID, hid_all, hidden)
    out = Gather(OUT, a_out, o_blk)

    def wrows(i, grp, half=None):
        if half is None:
            return w_o.at[ys[i], pl.ds(pl.multiple_of(grp * 64, 64), 64)]
        return w_o.at[ys[i], pl.ds(pl.multiple_of(grp * 64 + half * 32, 32), 32)]

    row_g = pl.multiple_of(g * 64, 64)
    send(W_Y, o_weight.at[pl.ds(row_g, 64), pl.ds(col_y[2], 2048)], wrows(0, g), dev_y[2])
    send(W_Y + 1, o_weight.at[pl.ds(row_g, 64), pl.ds(col_y[1], 2048)], wrows(0, g), dev_y[1])
    hid.first_own(0)
    send(W_Y + 2, o_weight.at[pl.ds(row_g, 32), pl.ds(col_y[3], 2048)], w_stage.at[0], dev_y[2])
    send(
        W_Y + 3,
        o_weight.at[pl.ds(pl.multiple_of(g * 64 + 32, 32), 32), pl.ds(col_y[3], 2048)],
        w_stage.at[1],
        dev_y[1],
    )
    hid.first_own(1)
    hid.second_own(1, 0)

    def w_spread(i):
        send(W_Z + 4 * i, wrows(i + 1, g), wrows(i + 1, g), dev_z[2])
        send(W_Z + 4 * i + 1, wrows(i + 1, g), wrows(i + 1, g), dev_z[1])
        send(W_SIB + 4 * i, wrows(i + 1, g), wrows(i + 1, g), dev_sib)

    def w_pass(i):
        got(W_Z + 4 * i, wrows(i + 1, gs[1]))
        send(W_Z + 4 * i + 2, wrows(i + 1, gs[1], 0), wrows(i + 1, gs[1], 0), dev_z[2])
        got(W_Z + 4 * i + 1, wrows(i + 1, gs[2]))
        send(W_Z + 4 * i + 3, wrows(i + 1, gs[2], 1), wrows(i + 1, gs[2], 1), dev_z[1])
        for s in (1, 2):
            send(W_SIB + 4 * i + s, wrows(i + 1, gs[s]), wrows(i + 1, gs[s]), dev_sib)

    def w_last(i):
        got(W_Z + 4 * i + 2, wrows(i + 1, gs[3], 0))
        got(W_Z + 4 * i + 3, wrows(i + 1, gs[3], 1))
        send(W_SIB + 4 * i + 3, wrows(i + 1, gs[3]), wrows(i + 1, gs[3]), dev_sib)

    l_qa.wait()
    l_oa.wait()
    l_qb.wait()
    l_ob.wait()

    def local_index(dest):
        def body(s, found):
            place = table[adapters[dest, s]]
            return jnp.where(lax.div(place, 8) == g, lax.rem(place, 8), found)

        return lax.fori_loop(0, 8, body, jnp.int32(0))

    def pack(d, carry):
        idx = local_index(mod(g + d, 8))
        send_a[d, :, 0:64] = qa_v[idx]
        send_a[d, :, 64:128] = oa_v[idx]
        send_b[d, 0:64, :] = qb_v[idx]
        send_b[d, 64:128, :] = ob_v[idx]
        return carry

    lax.fori_loop(0, 8, pack, 0)
    recv_a[g] = send_a[0]
    recv_b[g] = send_b[0]

    row = lax.broadcasted_iota(jnp.int32, (384, 128), 0)
    owner_v[...] = jnp.zeros((384, 128), jnp.int32)

    def mark(k, start):
        end = start + req_len[0, k]
        own = lax.div(table[adapters[g, req_slot[0, k]]], 8)
        owner_v[...] = jnp.where((row >= start) & (row < end), own, owner_v[...])
        return end

    lax.fori_loop(0, 16, mark, jnp.int32(0))

    hid.first_fwd(0)
    got(W_Y, wrows(1, g))
    w_spread(0)
    got(W_Y + 1, wrows(2, g))
    w_spread(1)
    got(W_Y + 2, w_stage.at[0])
    send(W_Y + 4, w_stage.at[0], wrows(1, g, 0), dev_y[2])
    got(W_Y + 3, w_stage.at[1])
    send(W_Y + 5, w_stage.at[1], wrows(2, g, 1), dev_y[1])
    l_attn.wait()
    send(ATT, attn, attn_all.at[y], dev_y[2])
    send(ATT + 1, attn, attn_all.at[y], dev_y[1])
    hid.first_fwd(1)
    hid.second_own(1, 1)
    hid.second_own(1, 2)
    hid.second_fwd(1, 0)
    w_pass(0)
    got(W_Y + 4, wrows(3, g, 0))
    got(W_Y + 5, wrows(3, g, 1))
    w_spread(2)
    w_pass(1)
    hid.second_fwd(1, 1)
    hid.second_fwd(1, 2)
    got(ATT, attn_all.at[ys[1]])
    send(ATT + 2, attn_all.at[ys[1], pl.ds(0, 192)], attn_all.at[ys[1], pl.ds(0, 192)], dev_y[2])
    got(ATT + 1, attn_all.at[ys[2]])
    send(ATT + 3, attn_all.at[ys[2], pl.ds(192, 192)], attn_all.at[ys[2], pl.ds(192, 192)], dev_y[1])
    hid.first_opp(1)
    hid.second_own(1, 3)
    hid.second_own(0, 0)
    hid.second_own(0, 1)
    hid.second_own(0, 2)
    hid.first_opp(0)
    hid.second_own(0, 3)
    w_last(0)
    w_pass(2)
    for d in range(1, 8):
        send(ADP_A + d, send_a.at[d], recv_a.at[g], {"group": mod(g + d, 8)})
    for d in range(1, 8):
        send(ADP_B + d, send_b.at[d], recv_b.at[g], {"group": mod(g + d, 8)})
    w_last(1)
    w_last(2)

    l_wo.wait()
    got(ATT + 2, attn_all.at[ys[3], pl.ds(0, 192)])
    got(ATT + 3, attn_all.at[ys[3], pl.ds(192, 192)])
    for i in range(3):
        for s in range(4):
            got(W_SIB + 4 * i + s, wrows(i + 1, gsib[s]))

    def partial(slot, xi):
        cols = pl.ds(pl.multiple_of(xs[xi] * 512, 512), 512)

        def half(h, carry):
            rows = pl.ds(pl.multiple_of(h * 192, 192), 192)
            total = jnp.dot(attn_all[0, rows, :], w_o[0, :, cols], preferred_element_type=F32)
            for i in range(1, 4):
                total = total + jnp.dot(attn_all[i, rows, :], w_o[i, :, cols], preferred_element_type=F32)
            part[slot, rows, :] = total
            return carry

        lax.fori_loop(0, 2, half, 0)

    upper, lower = pl.ds(0, 192), pl.ds(192, 192)
    partial(0, 3)
    send(RED, part.at[0, upper], r_opp.at[0], dev_x[2])
    send(RED + 1, part.at[0, lower], r_opp.at[1], dev_x[1])
    partial(1, 2)
    send(RED + 2, part.at[1, lower], r_nbr.at[0, lower], dev_x[2])
    partial(2, 1)
    send(RED + 3, part.at[2, upper], r_nbr.at[1, upper], dev_x[1])
    partial(3, 0)
    for i in range(4):
        hid.second_fwd(0, i)
    hid.second_fwd(1, 3)
    got(RED, r_opp.at[0])
    part[1, upper, :] = part[1, upper, :] + r_opp[0]
    send(RED + 4, part.at[1, upper], r_nbr.at[0, upper], dev_x[2])
    got(RED + 1, r_opp.at[1])
    part[2, lower, :] = part[2, lower, :] + r_opp[1]
    send(RED + 5, part.at[2, lower], r_nbr.at[1, lower], dev_x[1])

    l_hid.wait()
    for d in range(1, 8):
        got(ADP_A + d, recv_a.at[mod(g - d + 8, 8)])
    lane = lax.broadcasted_iota(jnp.int32, (384, 128), 1)
    down_v[...] = jnp.zeros((384, 128), F32)

    def down(o, carry):
        a = recv_a[o]
        from_hid = jnp.dot(hid_all[t], a, preferred_element_type=F32)
        from_att = jnp.dot(attn_all[y], a, preferred_element_type=F32)
        value = jnp.where(lane < 64, from_hid, from_att)
        down_v[...] = jnp.where(owner_v[...] == o, value, down_v[...])
        return carry

    lax.fori_loop(0, 8, down, 0)

    def piece(v):
        return pl.ds(pl.multiple_of(v * 96, 32), 96)

    y_off = [mod(y + d, 4) for d in range(4)]
    y_back = [mod(y - d + 4, 4) for d in range(4)]
    for d in (1, 2, 3):
        send(DOWN_1 + d - 1, down_v.at[piece(y_off[d])], down_1.at[d - 1], {"tensor": y_off[d] * 4 + x})
    for d in (1, 2, 3):
        got(DOWN_1 + d - 1, down_1.at[d - 1])
    down_s[0] = down_v[piece(y), :] + down_1[0] + down_1[1] + down_1[2]
    for d in (1, 2, 3):
        send(DOWN_2 + d - 1, down_s.at[0], down_2.at[d - 1], {"tensor": y * 4 + mod(x + d, 4)})
    for d in (1, 2, 3):
        got(DOWN_2 + d - 1, down_2.at[d - 1])
    down_s[1] = down_s[0] + down_2[0] + down_2[1] + down_2[2]
    for d in (1, 2, 3):
        send(DOWN_3 + d - 1, down_s.at[1], down_all.at[piece(y)], {"tensor": y_off[d] * 4 + x})
    down_all[piece(y), :] = down_s[1]
    for d in (1, 2, 3):
        got(DOWN_3 + d - 1, down_all.at[piece(y_back[d])])

    for d in range(1, 8):
        got(ADP_B + d, recv_b.at[mod(g - d + 8, 8)])
    up_q[...] = jnp.zeros((384, 512), F32)
    up_o[...] = jnp.zeros((384, 512), F32)

    def up(o, carry):
        b = recv_b[o]
        rows = jnp.where(owner_v[...] == o, down_all[...] * 0.5, 0.0)
        for keep, total in ((lane < 64, up_q), (lane >= 64, up_o)):
            kept = jnp.where(keep, rows, 0.0)
            high = kept.astype(BF16)
            low = (kept - high.astype(F32)).astype(BF16)
            total[...] += jnp.dot(high, b, preferred_element_type=F32) + jnp.dot(low, b, preferred_element_type=F32)
        return carry

    lax.fori_loop(0, 8, up, 0)
    part[3] = part[3] + up_o[...]

    for i in range(4):
        hid.second_opp(0, i)
        hid.second_opp(1, i)
    l_wq.wait()

    def query(k, carry):
        rows = pl.ds(pl.multiple_of(k * 512, 512), 512)
        up_q[...] += jnp.dot(hid_all[k], w_q[rows, :], preferred_element_type=F32)
        return carry

    lax.fori_loop(0, 16, query, 0)
    q_blk[...] = up_q[...].astype(BF16)
    s_q = load(8, q_blk, q_out)

    got(RED + 2, r_nbr.at[0, lower])
    got(RED + 3, r_nbr.at[1, upper])
    got(RED + 4, r_nbr.at[0, upper])
    got(RED + 5, r_nbr.at[1, lower])
    o_blk[...] = (part[3] + r_nbr[0] + r_nbr[1]).astype(BF16)
    s_o = load(9, o_blk, a_out.at[t])
    out.first_own(0)
    out.first_own(1)
    out.second_own(1, 0)
    out.second_own(0, 0)
    out.first_fwd(0)
    out.first_fwd(1)
    for i in (1, 2):
        out.second_own(0, i)
        out.second_own(1, i)
    out.second_fwd(0, 0)
    out.second_fwd(1, 0)
    out.first_opp(0)
    out.second_own(0, 3)
    out.first_opp(1)
    out.second_own(1, 3)
    for i in (1, 2, 3):
        out.second_fwd(0, i)
        out.second_fwd(1, i)
    for i in range(4):
        out.second_opp(0, i)
        out.second_opp(1, i)
    for copy in sent:
        copy.wait_send()
    s_q.wait()
    s_o.wait()


def body(hidden, attn, q_weight, o_weight, table, adapters, req_slot, req_len, qa, qb, oa, ob):
    hbm = pl.BlockSpec(memory_space=pl.ANY)
    smem = pl.BlockSpec(memory_space=pltpu.SMEM)
    vm = pltpu.VMEM
    queries, blocks = pl.pallas_call(
        kernel,
        out_shape=(
            jax.ShapeDtypeStruct((384, 512), BF16),
            jax.ShapeDtypeStruct((16, 384, 512), BF16),
        ),
        in_specs=[hbm] * 8 + [smem] * 4,
        out_specs=(hbm, hbm),
        scratch_shapes=[
            vm((16, 384, 512), BF16),
            vm((4, 384, 512), BF16),
            vm((4, 512, 2048), BF16),
            vm((2, 32, 2048), BF16),
            vm((8192, 512), BF16),
            vm((8, 512, 64), BF16),
            vm((8, 64, 512), BF16),
            vm((8, 512, 64), BF16),
            vm((8, 64, 512), BF16),
            vm((8, 512, 128), BF16),
            vm((8, 128, 512), BF16),
            vm((8, 512, 128), BF16),
            vm((8, 128, 512), BF16),
            vm((384, 128), jnp.int32),
            vm((384, 128), F32),
            vm((3, 96, 128), F32),
            vm((3, 96, 128), F32),
            vm((2, 96, 128), F32),
            vm((384, 128), F32),
            vm((384, 512), F32),
            vm((384, 512), F32),
            vm((4, 384, 512), F32),
            vm((2, 192, 512), F32),
            vm((2, 384, 512), F32),
            vm((384, 512), BF16),
            vm((384, 512), BF16),
            pltpu.SemaphoreType.DMA((N_SEMS,)),
            pltpu.SemaphoreType.DMA((N_SEMS,)),
            pltpu.SemaphoreType.DMA((N_LOCAL,)),
        ],
        compiler_params=pltpu.CompilerParams(
            collective_id=0, has_side_effects=True, vmem_limit_bytes=60 * 1024 * 1024
        ),
    )(hidden, attn, q_weight, o_weight, qa, qb, oa, ob, table, adapters, req_slot, req_len)
    return queries, jnp.transpose(blocks, (1, 0, 2)).reshape(384, 8192)


def solution(mesh):
    return jax.shard_map(
        body,
        mesh=mesh,
        in_specs=(
            P("group", "tensor"),
            P("group", "tensor"),
            P(None, "tensor"),
            P("tensor", None),
            P(),
            P(),
            P("group", None),
            P("group", None),
            P("group", "tensor", None),
            P("group", None, "tensor"),
            P("group", "tensor", None),
            P("group", None, "tensor"),
        ),
        out_specs=(P("group", "tensor"), P("group", None)),
        check_vma=False,
    )
```

```python
import jax
import jax.numpy as jnp
from jax import lax
from jax.experimental import pallas as pl
from jax.experimental.pallas import tpu as pltpu
from jax.sharding import PartitionSpec as P

MESH = pl.DeviceIdType.MESH
F32 = jnp.float32
BF16 = jnp.bfloat16

W_Y = 0
W_Z = 6
W_SIB = 18
ATT = 30
ADP = 34
DOWN_1 = 42
DOWN_2 = 45
DOWN_3 = 48
RED = 51
HID = 57
OUT = 97
N_SEMS = 137
N_LOCAL = 8


def mod(a, n):
    return lax.rem(a + n, n)


def kernel(
    hidden, attn, q_weight, o_weight, qa, qb, oa, ob, table, adapters, req_slot, req_len,
    q_out, a_out,
    hid_all, attn_all, w_o, w_stage, w_q, qa_v, qb_v, oa_v, ob_v, send_a, recv_a,
    owner_v, down_v, down_1, down_2, down_s, down_all, up_q, up_o, part, r_opp, r_nbr,
    send_sem, recv_sem, local_sem,
):
    g = lax.axis_index("group")
    t = lax.axis_index("tensor")
    z, c = lax.div(g, 2), lax.rem(g, 2)
    y, x = lax.div(t, 4), lax.rem(t, 4)
    ys = [y, mod(y - 1, 4), mod(y + 1, 4), mod(y + 2, 4)]
    xs = [x, mod(x - 1, 4), mod(x + 1, 4), mod(x + 2, 4)]
    gs = [g] + [mod(z + d, 4) * 2 + c for d in (-1, 1, 2)]
    sib = z * 2 + (1 - c)
    gsib = [sib] + [mod(z + d, 4) * 2 + (1 - c) for d in (-1, 1, 2)]
    dev_x = [None] + [{"tensor": y * 4 + xs[i]} for i in (1, 2, 3)]
    dev_y = [None] + [{"tensor": ys[i] * 4 + x} for i in (1, 2, 3)]
    dev_z = [None] + [{"group": gs[i]} for i in (1, 2)]
    dev_sib = {"group": sib}

    sent = []

    def send(k, src, dst, dev):
        copy = pltpu.make_async_remote_copy(
            src_ref=src, dst_ref=dst, send_sem=send_sem.at[k], recv_sem=recv_sem.at[k],
            device_id=dev, device_id_type=MESH,
        )
        copy.start()
        sent.append(copy)

    def got(k, ref):
        pltpu.make_async_remote_copy(
            src_ref=ref, dst_ref=ref, send_sem=send_sem.at[k], recv_sem=recv_sem.at[k],
            device_id=dev_sib, device_id_type=MESH,
        ).wait_recv()

    def load(k, src, dst):
        copy = pltpu.make_async_copy(src, dst, local_sem.at[k])
        copy.start()
        return copy

    barrier = pltpu.get_barrier_semaphore()
    for i in (1, 2, 3):
        pl.semaphore_signal(barrier, inc=1, device_id=dev_x[i], device_id_type=MESH)
        pl.semaphore_signal(barrier, inc=1, device_id=dev_y[i], device_id_type=MESH)
    for d in range(1, 8):
        pl.semaphore_signal(barrier, inc=1, device_id={"group": mod(g + d, 8)}, device_id_type=MESH)
    col_y = [pl.multiple_of(v * 2048, 2048) for v in ys]
    l_qa, l_oa = load(0, qa, qa_v), load(1, oa, oa_v)
    l_qb, l_ob = load(2, qb, qb_v), load(3, ob, ob_v)
    l_attn = load(4, attn, attn_all.at[y])
    l_hid = load(5, hidden, hid_all.at[t])
    l_wo = load(6, o_weight.at[:, pl.ds(col_y[0], 2048)], w_o.at[y])
    l_wq = load(7, q_weight, w_q)
    pl.semaphore_wait(barrier, 13)

    class Gather:
        def __init__(self, base, buf, own):
            self.base, self.buf, self.own = base, buf, own

        def block(self, half, i, j):
            return ys[j] * 4 + xs[i] if half == 0 else ys[i] * 4 + xs[j]

        def devs(self, half):
            return (dev_x, dev_y) if half == 0 else (dev_y, dev_x)

        def rows(self, half, i, j, quarter=None):
            b = self.block(half, i, j)
            start, size = (half * 192, 192) if quarter is None else (half * 192 + quarter * 96, 96)
            if len(self.buf.shape) == 3:
                return self.buf.at[b, pl.ds(start, size)]
            return self.buf.at[pl.ds(start, size), pl.ds(pl.multiple_of(b * 512, 512), 512)]

        def src_own(self, half):
            return self.own.at[pl.ds(half * 192, 192)]

        def first_own(self, half):
            dev = self.devs(half)[0]
            k = self.base + half * 20
            send(k, self.src_own(half), self.rows(half, 0, 0), dev[2])
            send(k + 1, self.src_own(half), self.rows(half, 0, 0), dev[1])

        def first_fwd(self, half):
            dev = self.devs(half)[0]
            k = self.base + half * 20
            got(k, self.rows(half, 1, 0))
            send(k + 2, self.rows(half, 1, 0, 0), self.rows(half, 1, 0, 0), dev[2])
            got(k + 1, self.rows(half, 2, 0))
            send(k + 3, self.rows(half, 2, 0, 1), self.rows(half, 2, 0, 1), dev[1])

        def first_opp(self, half):
            k = self.base + half * 20
            got(k + 2, self.rows(half, 3, 0, 0))
            got(k + 3, self.rows(half, 3, 0, 1))

        def second_own(self, half, i):
            dev = self.devs(half)[1]
            k = self.base + half * 20 + 4 + 4 * i
            src = self.src_own(half) if i == 0 else self.rows(half, i, 0)
            send(k, src, self.rows(half, i, 0), dev[2])
            send(k + 1, src, self.rows(half, i, 0), dev[1])

        def second_fwd(self, half, i):
            dev = self.devs(half)[1]
            k = self.base + half * 20 + 4 + 4 * i
            got(k, self.rows(half, i, 1))
            send(k + 2, self.rows(half, i, 1, 0), self.rows(half, i, 1, 0), dev[2])
            got(k + 1, self.rows(half, i, 2))
            send(k + 3, self.rows(half, i, 2, 1), self.rows(half, i, 2, 1), dev[1])

        def second_opp(self, half, i):
            k = self.base + half * 20 + 4 + 4 * i
            got(k + 2, self.rows(half, i, 3, 0))
            got(k + 3, self.rows(half, i, 3, 1))

    hid = Gather(HID, hid_all, hidden)
    out = Gather(OUT, a_out, a_out.at[:, pl.ds(pl.multiple_of(t * 512, 512), 512)])

    def wrows(i, grp, half=None):
        if half is None:
            return w_o.at[ys[i], pl.ds(pl.multiple_of(grp * 64, 64), 64)]
        return w_o.at[ys[i], pl.ds(pl.multiple_of(grp * 64 + half * 32, 32), 32)]

    row_g = pl.multiple_of(g * 64, 64)
    send(W_Y, o_weight.at[pl.ds(row_g, 64), pl.ds(col_y[2], 2048)], wrows(0, g), dev_y[2])
    send(W_Y + 1, o_weight.at[pl.ds(row_g, 64), pl.ds(col_y[1], 2048)], wrows(0, g), dev_y[1])
    hid.first_own(0)
    send(W_Y + 2, o_weight.at[pl.ds(row_g, 32), pl.ds(col_y[3], 2048)], w_stage.at[0], dev_y[2])
    send(
        W_Y + 3,
        o_weight.at[pl.ds(pl.multiple_of(g * 64 + 32, 32), 32), pl.ds(col_y[3], 2048)],
        w_stage.at[1],
        dev_y[1],
    )
    hid.first_own(1)
    hid.second_own(1, 0)

    def w_spread(i):
        send(W_Z + 4 * i, wrows(i + 1, g), wrows(i + 1, g), dev_z[2])
        send(W_Z + 4 * i + 1, wrows(i + 1, g), wrows(i + 1, g), dev_z[1])
        send(W_SIB + 4 * i, wrows(i + 1, g), wrows(i + 1, g), dev_sib)

    def w_pass(i):
        got(W_Z + 4 * i, wrows(i + 1, gs[1]))
        send(W_Z + 4 * i + 2, wrows(i + 1, gs[1], 0), wrows(i + 1, gs[1], 0), dev_z[2])
        got(W_Z + 4 * i + 1, wrows(i + 1, gs[2]))
        send(W_Z + 4 * i + 3, wrows(i + 1, gs[2], 1), wrows(i + 1, gs[2], 1), dev_z[1])
        for s in (1, 2):
            send(W_SIB + 4 * i + s, wrows(i + 1, gs[s]), wrows(i + 1, gs[s]), dev_sib)

    def w_last(i):
        got(W_Z + 4 * i + 2, wrows(i + 1, gs[3], 0))
        got(W_Z + 4 * i + 3, wrows(i + 1, gs[3], 1))
        send(W_SIB + 4 * i + 3, wrows(i + 1, gs[3]), wrows(i + 1, gs[3]), dev_sib)

    l_qa.wait()
    l_oa.wait()
    l_qb.wait()
    l_ob.wait()

    def local_index(dest):
        def body(s, found):
            place = table[adapters[dest, s]]
            return jnp.where(lax.div(place, 8) == g, lax.rem(place, 8), found)

        return lax.fori_loop(0, 8, body, jnp.int32(0))

    def pack(d, carry):
        idx = local_index(mod(g + d, 8))
        send_a[d, 0:64, :] = qa_v[idx]
        send_a[d, 64:128, :] = oa_v[idx]
        send_a[d, 128:192, :] = qb_v[idx]
        send_a[d, 192:256, :] = ob_v[idx]
        return carry

    lax.fori_loop(0, 8, pack, 0)
    recv_a[g] = send_a[0]

    row = lax.broadcasted_iota(jnp.int32, (384, 128), 0)
    owner_v[...] = jnp.zeros((384, 128), jnp.int32)

    def mark(k, start):
        end = start + req_len[0, k]
        own = lax.div(table[adapters[g, req_slot[0, k]]], 8)
        owner_v[...] = jnp.where((row >= start) & (row < end), own, owner_v[...])
        return end

    lax.fori_loop(0, 16, mark, jnp.int32(0))

    hid.first_fwd(0)
    got(W_Y, wrows(1, g))
    w_spread(0)
    got(W_Y + 1, wrows(2, g))
    w_spread(1)
    got(W_Y + 2, w_stage.at[0])
    send(W_Y + 4, w_stage.at[0], wrows(1, g, 0), dev_y[2])
    got(W_Y + 3, w_stage.at[1])
    send(W_Y + 5, w_stage.at[1], wrows(2, g, 1), dev_y[1])
    l_attn.wait()
    send(ATT, attn, attn_all.at[y], dev_y[2])
    send(ATT + 1, attn, attn_all.at[y], dev_y[1])
    hid.first_fwd(1)
    hid.second_own(1, 1)
    hid.second_own(1, 2)
    hid.second_fwd(1, 0)
    w_pass(0)
    got(W_Y + 4, wrows(3, g, 0))
    got(W_Y + 5, wrows(3, g, 1))
    w_spread(2)
    w_pass(1)
    hid.second_fwd(1, 1)
    hid.second_fwd(1, 2)
    got(ATT, attn_all.at[ys[1]])
    send(ATT + 2, attn_all.at[ys[1], pl.ds(0, 192)], attn_all.at[ys[1], pl.ds(0, 192)], dev_y[2])
    got(ATT + 1, attn_all.at[ys[2]])
    send(ATT + 3, attn_all.at[ys[2], pl.ds(192, 192)], attn_all.at[ys[2], pl.ds(192, 192)], dev_y[1])
    hid.first_opp(1)
    hid.second_own(1, 3)
    hid.second_own(0, 0)
    hid.second_own(0, 1)
    hid.second_own(0, 2)
    hid.first_opp(0)
    hid.second_own(0, 3)
    w_last(0)
    w_pass(2)
    for d in range(1, 8):
        send(ADP + d, send_a.at[d], recv_a.at[g], {"group": mod(g + d, 8)})
    w_last(1)
    w_last(2)

    l_wo.wait()
    got(ATT + 2, attn_all.at[ys[3], pl.ds(0, 192)])
    got(ATT + 3, attn_all.at[ys[3], pl.ds(192, 192)])
    for i in range(3):
        for s in range(4):
            got(W_SIB + 4 * i + s, wrows(i + 1, gsib[s]))

    def partial(slot, xi):
        cols = pl.ds(pl.multiple_of(xs[xi] * 512, 512), 512)

        def half(h, carry):
            rows = pl.ds(pl.multiple_of(h * 192, 192), 192)
            total = jnp.dot(attn_all[0, rows, :], w_o[0, :, cols], preferred_element_type=F32)
            for i in range(1, 4):
                total = total + jnp.dot(attn_all[i, rows, :], w_o[i, :, cols], preferred_element_type=F32)
            part[slot, rows, :] = total
            return carry

        lax.fori_loop(0, 2, half, 0)

    upper, lower = pl.ds(0, 192), pl.ds(192, 192)
    partial(0, 3)
    send(RED, part.at[0, upper], r_opp.at[0], dev_x[2])
    send(RED + 1, part.at[0, lower], r_opp.at[1], dev_x[1])
    partial(1, 2)
    send(RED + 2, part.at[1, lower], r_nbr.at[0, lower], dev_x[2])
    partial(2, 1)
    send(RED + 3, part.at[2, upper], r_nbr.at[1, upper], dev_x[1])
    partial(3, 0)
    for i in range(4):
        hid.second_fwd(0, i)
    hid.second_fwd(1, 3)
    got(RED, r_opp.at[0])
    part[1, upper, :] = part[1, upper, :] + r_opp[0]
    send(RED + 4, part.at[1, upper], r_nbr.at[0, upper], dev_x[2])
    got(RED + 1, r_opp.at[1])
    part[2, lower, :] = part[2, lower, :] + r_opp[1]
    send(RED + 5, part.at[2, lower], r_nbr.at[1, lower], dev_x[1])

    l_hid.wait()
    for d in range(1, 8):
        got(ADP + d, recv_a.at[mod(g - d + 8, 8)])
    lane = lax.broadcasted_iota(jnp.int32, (384, 128), 1)
    down_v[...] = jnp.zeros((384, 128), F32)

    def down(o, carry):
        a = recv_a[o, 0:128, :]
        from_hid = lax.dot_general(hid_all[t], a, (((1,), (1,)), ((), ())), preferred_element_type=F32)
        from_att = lax.dot_general(attn_all[y], a, (((1,), (1,)), ((), ())), preferred_element_type=F32)
        value = jnp.where(lane < 64, from_hid, from_att)
        down_v[...] = jnp.where(owner_v[...] == o, value, down_v[...])
        return carry

    lax.fori_loop(0, 8, down, 0)

    def piece(v):
        return pl.ds(pl.multiple_of(v * 96, 32), 96)

    y_off = [mod(y + d, 4) for d in range(4)]
    y_back = [mod(y - d + 4, 4) for d in range(4)]
    for d in (1, 2, 3):
        send(DOWN_1 + d - 1, down_v.at[piece(y_off[d])], down_1.at[d - 1], {"tensor": y_off[d] * 4 + x})
    for d in (1, 2, 3):
        got(DOWN_1 + d - 1, down_1.at[d - 1])
    down_s[0] = down_v[piece(y), :] + down_1[0] + down_1[1] + down_1[2]
    for d in (1, 2, 3):
        send(DOWN_2 + d - 1, down_s.at[0], down_2.at[d - 1], {"tensor": y * 4 + mod(x + d, 4)})
    for d in (1, 2, 3):
        got(DOWN_2 + d - 1, down_2.at[d - 1])
    down_s[1] = down_s[0] + down_2[0] + down_2[1] + down_2[2]
    for d in (1, 2, 3):
        send(DOWN_3 + d - 1, down_s.at[1], down_all.at[piece(y)], {"tensor": y_off[d] * 4 + x})
    down_all[piece(y), :] = down_s[1]
    for d in (1, 2, 3):
        got(DOWN_3 + d - 1, down_all.at[piece(y_back[d])])

    up_q[...] = jnp.zeros((384, 512), F32)
    up_o[...] = jnp.zeros((384, 512), F32)

    def up(o, carry):
        b = recv_a[o, 128:256, :]
        rows = jnp.where(owner_v[...] == o, down_all[...] * 0.5, 0.0)
        for keep, total in ((lane < 64, up_q), (lane >= 64, up_o)):
            kept = jnp.where(keep, rows, 0.0)
            high = kept.astype(BF16)
            low = (kept - high.astype(F32)).astype(BF16)
            total[...] += jnp.dot(high, b, preferred_element_type=F32) + jnp.dot(low, b, preferred_element_type=F32)
        return carry

    lax.fori_loop(0, 8, up, 0)
    part[3] = part[3] + up_o[...]

    for i in range(4):
        hid.second_opp(0, i)
        hid.second_opp(1, i)
    l_wq.wait()

    def query(k, carry):
        rows = pl.ds(pl.multiple_of(k * 512, 512), 512)
        up_q[...] += jnp.dot(hid_all[k], w_q[rows, :], preferred_element_type=F32)
        return carry

    lax.fori_loop(0, 16, query, 0)
    q_out[...] = up_q[...].astype(BF16)

    got(RED + 2, r_nbr.at[0, lower])
    got(RED + 3, r_nbr.at[1, upper])
    got(RED + 4, r_nbr.at[0, upper])
    got(RED + 5, r_nbr.at[1, lower])
    own_cols = pl.ds(pl.multiple_of(t * 512, 512), 512)
    a_out[:, own_cols] = (part[3] + r_nbr[0] + r_nbr[1]).astype(BF16)
    out.first_own(0)
    out.first_own(1)
    out.second_own(1, 0)
    out.second_own(0, 0)
    out.first_fwd(0)
    out.first_fwd(1)
    for i in (1, 2):
        out.second_own(0, i)
        out.second_own(1, i)
    out.second_fwd(0, 0)
    out.second_fwd(1, 0)
    out.first_opp(0)
    out.second_own(0, 3)
    out.first_opp(1)
    out.second_own(1, 3)
    for i in (1, 2, 3):
        out.second_fwd(0, i)
        out.second_fwd(1, i)
    for i in range(4):
        out.second_opp(0, i)
        out.second_opp(1, i)
    for copy in sent:
        copy.wait_send()


def body(hidden, attn, q_weight, o_weight, table, adapters, req_slot, req_len, qa, qb, oa, ob):
    hbm = pl.BlockSpec(memory_space=pl.ANY)
    smem = pl.BlockSpec(memory_space=pltpu.SMEM)
    vm = pltpu.VMEM
    qa_t, oa_t = jnp.transpose(qa, (0, 2, 1)), jnp.transpose(oa, (0, 2, 1))
    return pl.pallas_call(
        kernel,
        out_shape=(
            vm((384, 512), BF16),
            vm((384, 8192), BF16),
        ),
        in_specs=[hbm] * 8 + [smem] * 4,
        out_specs=[pl.BlockSpec(memory_space=pltpu.VMEM)] * 2,
        scratch_shapes=[
            vm((16, 384, 512), BF16),
            vm((4, 384, 512), BF16),
            vm((4, 512, 2048), BF16),
            vm((2, 32, 2048), BF16),
            vm((8192, 512), BF16),
            vm((8, 64, 512), BF16),
            vm((8, 64, 512), BF16),
            vm((8, 64, 512), BF16),
            vm((8, 64, 512), BF16),
            vm((8, 256, 512), BF16),
            vm((8, 256, 512), BF16),
            vm((384, 128), jnp.int32),
            vm((384, 128), F32),
            vm((3, 96, 128), F32),
            vm((3, 96, 128), F32),
            vm((2, 96, 128), F32),
            vm((384, 128), F32),
            vm((384, 512), F32),
            vm((384, 512), F32),
            vm((4, 384, 512), F32),
            vm((2, 192, 512), F32),
            vm((2, 384, 512), F32),
            pltpu.SemaphoreType.DMA((N_SEMS,)),
            pltpu.SemaphoreType.DMA((N_SEMS,)),
            pltpu.SemaphoreType.DMA((N_LOCAL,)),
        ],
        compiler_params=pltpu.CompilerParams(
            collective_id=0, has_side_effects=True, vmem_limit_bytes=48 * 1024 * 1024
        ),
    )(hidden, attn, q_weight, o_weight, qa_t, qb, oa_t, ob, table, adapters, req_slot, req_len)


def solution(mesh):
    return jax.shard_map(
        body,
        mesh=mesh,
        in_specs=(
            P("group", "tensor"),
            P("group", "tensor"),
            P(None, "tensor"),
            P("tensor", None),
            P(),
            P(),
            P("group", None),
            P("group", None),
            P("group", "tensor", None),
            P("group", None, "tensor"),
            P("group", "tensor", None),
            P("group", None, "tensor"),
        ),
        out_specs=(P("group", "tensor"), P("group", None)),
        check_vma=False,
    )
```

```python
import jax
import jax.numpy as jnp
from jax import lax
from jax.experimental import pallas as pl
from jax.experimental.pallas import tpu as pltpu
from jax.sharding import PartitionSpec as P

MESH = pl.DeviceIdType.MESH
F32 = jnp.float32
BF16 = jnp.bfloat16

N_RECV = 58
N_SEND = 4
N_LOCAL = 7


def mod(a, n):
    return lax.rem(a + n, n)


def kernel(
    hidden, attn, q_weight, o_weight, qa, qb, oa, ob, table, adapters, req_slot, req_len,
    q_out, a_out,
    hid_all, attn_all, w_o, w_stage, w_q, qa_v, qb_v, oa_v, ob_v, send_a, recv_a,
    owner_v, down_v, down_1, down_2, down_s, down_all, up_q, up_o, part, r_opp, r_nbr, o_blk, q_blk,
    send_sem, recv_sem, local_sem,
):
    g = lax.axis_index("group")
    t = lax.axis_index("tensor")
    z, c = lax.div(g, 2), lax.rem(g, 2)
    y, x = lax.div(t, 4), lax.rem(t, 4)
    ys = [y, mod(y - 1, 4), mod(y + 1, 4), mod(y + 2, 4)]
    xs = [x, mod(x - 1, 4), mod(x + 1, 4), mod(x + 2, 4)]
    gs = [g] + [mod(z + d, 4) * 2 + c for d in (-1, 1, 2)]
    sib = z * 2 + (1 - c)
    dev_x = [None] + [{"tensor": y * 4 + xs[i]} for i in (1, 2, 3)]
    dev_y = [None] + [{"tensor": ys[i] * 4 + x} for i in (1, 2, 3)]
    dev_z = [None] + [{"group": gs[i]} for i in (1, 2)]
    dev_sib = {"group": sib}

    names, expected, leaving = {}, {}, {}

    def size(ref):
        count = 1
        for extent in ref.shape:
            count *= extent
        return count * ref.dtype.itemsize

    def wait_bytes(sem, count):
        rows = w_q.at[pl.ds(0, count // 1024)]
        pltpu.make_async_copy(rows, rows, sem).wait()

    def send(name, lot, src, dst, dev):
        k = names.setdefault(name, len(names))
        pltpu.make_async_remote_copy(
            src_ref=src, dst_ref=dst, send_sem=send_sem.at[lot], recv_sem=recv_sem.at[k],
            device_id=dev, device_id_type=MESH,
        ).start()
        expected[name] = expected.get(name, 0) + size(src)
        leaving[lot] = leaving.get(lot, 0) + size(src)

    def got(name):
        wait_bytes(recv_sem.at[names[name]], expected.pop(name))

    def gone(lot):
        wait_bytes(send_sem.at[lot], leaving.pop(lot))

    def load(k, src, dst):
        pltpu.make_async_copy(src, dst, local_sem.at[k]).start()
        return size(src)

    def loaded(k, count):
        wait_bytes(local_sem.at[k], count)

    barrier = pltpu.get_barrier_semaphore()
    for i in (1, 2, 3):
        pl.semaphore_signal(barrier, inc=1, device_id=dev_x[i], device_id_type=MESH)
        pl.semaphore_signal(barrier, inc=1, device_id=dev_y[i], device_id_type=MESH)
    for d in range(1, 8):
        pl.semaphore_signal(barrier, inc=1, device_id={"group": mod(g + d, 8)}, device_id_type=MESH)
    l_adp = load(0, qa, qa_v) + load(0, oa, oa_v) + load(0, qb, qb_v) + load(0, ob, ob_v)
    l_hid = load(1, hidden, hid_all.at[t])
    l_attn = load(2, attn, attn_all.at[y])
    x_slot = [xs[3], xs[2], xs[1], xs[0]]

    def wcols(i, j):
        return pl.ds(pl.multiple_of(ys[i] * 2048 + x_slot[j] * 512, 512), 512)

    l_wo = sum(load(3, o_weight.at[:, wcols(0, j)], w_o.at[y, j]) for j in range(4))

    def local_index(dest):
        def body(s, found):
            place = table[adapters[dest, s]]
            return jnp.where(lax.div(place, 8) == g, lax.rem(place, 8), found)

        return lax.fori_loop(0, 8, body, jnp.int32(0))

    def pack_adapters():
        loaded(0, l_adp)

        def pack(d, carry):
            idx = local_index(mod(g + d, 8))
            send_a[d, 0:64, :] = qa_v[idx]
            send_a[d, 64:128, :] = oa_v[idx]
            send_a[d, 128:192, :] = qb_v[idx]
            send_a[d, 192:256, :] = ob_v[idx]
            return carry

        lax.fori_loop(0, 8, pack, 0)
        recv_a[g] = send_a[0]

    def mark_rows():
        row = lax.broadcasted_iota(jnp.int32, (384, 128), 0)
        owner_v[...] = jnp.zeros((384, 128), jnp.int32)

        def mark(k, start):
            end = start + req_len[0, k]
            own = lax.div(table[adapters[g, req_slot[0, k]]], 8)
            owner_v[...] = jnp.where((row >= start) & (row < end), own, owner_v[...])
            return end

        lax.fori_loop(0, 16, mark, jnp.int32(0))

    pl.semaphore_wait(barrier, 13)

    class Gather:
        def __init__(self, name, lot, buf, own):
            self.name, self.lot, self.buf, self.own = name, lot, buf, own

        def block(self, half, i, j):
            return ys[j] * 4 + xs[i] if half == 0 else ys[i] * 4 + xs[j]

        def devs(self, half):
            return (dev_x, dev_y) if half == 0 else (dev_y, dev_x)

        def rows(self, half, i, j, quarter=None):
            b = self.block(half, i, j)
            start, size = (half * 192, 192) if quarter is None else (half * 192 + quarter * 96, 96)
            if len(self.buf.shape) == 3:
                return self.buf.at[b, pl.ds(start, size)]
            return self.buf.at[pl.ds(start, size), pl.ds(pl.multiple_of(b * 512, 512), 512)]

        def src_own(self, half):
            return self.own.at[pl.ds(half * 192, 192)]

        def key(self, *what):
            return (self.name,) + what

        def first_own(self, half):
            dev = self.devs(half)[0]
            for to in (2, 1):
                send(self.key(half, "own"), self.lot, self.src_own(half), self.rows(half, 0, 0), dev[to])

        def first_fwd(self, half):
            dev = self.devs(half)[0]
            got(self.key(half, "own"))
            for way in (0, 1):
                ref = self.rows(half, 1 + way, 0, way)
                send(self.key(half, "opp"), self.lot, ref, ref, dev[2 - way])

        def first_opp(self, half):
            got(self.key(half, "opp"))

        def second_own(self, half, i):
            dev = self.devs(half)[1]
            src = self.src_own(half) if i == 0 else self.rows(half, i, 0)
            for to in (2, 1):
                send(self.key(half, i), self.lot, src, self.rows(half, i, 0), dev[to])

        def second_fwd(self, half, i):
            dev = self.devs(half)[1]
            got(self.key(half, i))
            for way in (0, 1):
                ref = self.rows(half, i, 1 + way, way)
                send(self.key("last"), self.lot, ref, ref, dev[2 - way])

        def last(self):
            got(self.key("last"))

    hid = Gather("hid", 2, hid_all, hidden)
    out = Gather("out", 3, a_out, o_blk)

    def wrows(i, ch, grp, half=None):
        if half is None:
            return w_o.at[ys[i], pl.ds(2 * ch, 2), pl.ds(pl.multiple_of(grp * 64, 64), 64)]
        return w_o.at[ys[i], pl.ds(2 * ch, 2), pl.ds(pl.multiple_of(grp * 64 + half * 32, 32), 32)]

    def wrow(i, j, grp):
        return w_o.at[ys[i], j, pl.ds(pl.multiple_of(grp * 64, 64), 64)]

    def w_first(ch):
        for j in (2 * ch, 2 * ch + 1):
            for way, to in ((0, 2), (1, 1)):
                rows = pl.ds(pl.multiple_of(g * 64, 64), 64)
                send(("nbr", ch, way), 0, o_weight.at[rows, wcols(to, j)], wrow(0, j, g), dev_y[to])
                rows = pl.ds(pl.multiple_of(g * 64 + way * 32, 32), 32)
                send(("opp", ch), 0, o_weight.at[rows, wcols(3, j)], w_stage.at[way, j], dev_y[to])

    def w_second(ch):
        got(("opp", ch))
        for way in (0, 1):
            send(("opp2", ch), 0, w_stage.at[way, pl.ds(2 * ch, 2)], wrows(1 + way, ch, g, way), dev_y[2 - way])

    def w_spread(ch, i):
        got(("nbr", ch, i) if i < 2 else ("opp2", ch))
        ref = wrows(i + 1, ch, g)
        send(("z", ch, i), 0, ref, ref, dev_z[2])
        send(("z", ch, i), 0, ref, ref, dev_z[1])
        send(("sib", ch), 0, ref, ref, dev_sib)

    def w_pass(ch, i):
        got(("z", ch, i))
        for way in (0, 1):
            ref = wrows(i + 1, ch, gs[1 + way], way)
            send(("zopp", ch), 0, ref, ref, dev_z[2 - way])
        for way in (0, 1):
            ref = wrows(i + 1, ch, gs[1 + way])
            send(("sib", ch), 0, ref, ref, dev_sib)

    def w_last(ch):
        got(("zopp", ch))
        for i in range(3):
            ref = wrows(i + 1, ch, gs[3])
            send(("sib", ch), 0, ref, ref, dev_sib)

    def w_done(ch):
        got(("sib", ch))

    def adapters_send(name, first):
        for d in (4, 2, 6, 1, 3, 5, 7):
            rows = pl.ds(first, 128)
            send(name, 1, send_a.at[d, rows], recv_a.at[g, rows], {"group": mod(g + d, 8)})

    upper, lower = pl.ds(0, 192), pl.ds(192, 192)

    def attn_own():
        for to in (2, 1):
            send("attn", 2, attn, attn_all.at[y], dev_y[to])

    def attn_fwd():
        got("attn")
        for way, part_rows in ((0, upper), (1, lower)):
            ref = attn_all.at[ys[1 + way], part_rows]
            send("attn_opp", 2, ref, ref, dev_y[2 - way])

    def partial(j):
        def half(h, carry):
            rows = pl.ds(pl.multiple_of(h * 192, 192), 192)
            total = jnp.dot(attn_all[0, rows, :], w_o[0, j], preferred_element_type=F32)
            for i in range(1, 4):
                total = total + jnp.dot(attn_all[i, rows, :], w_o[i, j], preferred_element_type=F32)
            part[j, rows, :] = total
            return carry

        lax.fori_loop(0, 2, half, 0)

    lane = lax.broadcasted_iota(jnp.int32, (384, 128), 1)
    y_off = [mod(y + d, 4) for d in range(4)]

    def piece(v):
        return pl.ds(pl.multiple_of(v * 96, 32), 96)

    def down_product():
        down_v[...] = jnp.zeros((384, 128), F32)

        def down(o, carry):
            a = recv_a[o, 0:128, :]
            from_hid = lax.dot_general(hid_all[t], a, (((1,), (1,)), ((), ())), preferred_element_type=F32)
            from_att = lax.dot_general(attn_all[y], a, (((1,), (1,)), ((), ())), preferred_element_type=F32)
            value = jnp.where(lane < 64, from_hid, from_att)
            down_v[...] = jnp.where(owner_v[...] == o, value, down_v[...])
            return carry

        lax.fori_loop(0, 8, down, 0)
        for d in (1, 2, 3):
            send("down1", 1, down_v.at[piece(y_off[d])], down_1.at[d - 1], {"tensor": y_off[d] * 4 + x})

    def down_across():
        got("down1")
        down_s[0] = down_v[piece(y), :] + down_1[0] + down_1[1] + down_1[2]
        for d in (1, 2, 3):
            send("down2", 1, down_s.at[0], down_2.at[d - 1], {"tensor": y * 4 + mod(x + d, 4)})

    def down_back():
        got("down2")
        down_s[1] = down_s[0] + down_2[0] + down_2[1] + down_2[2]
        for d in (1, 2, 3):
            send("down3", 1, down_s.at[1], down_all.at[piece(y)], {"tensor": y_off[d] * 4 + x})
        down_all[piece(y), :] = down_s[1]

    def up_product():
        up_q[...] = jnp.zeros((384, 512), F32)
        up_o[...] = jnp.zeros((384, 512), F32)

        def up(o, carry):
            b = recv_a[o, 128:256, :]
            rows = jnp.where(owner_v[...] == o, down_all[...] * 0.5, 0.0)
            for keep, total in ((lane < 64, up_q), (lane >= 64, up_o)):
                kept = jnp.where(keep, rows, 0.0)
                high = kept.astype(BF16)
                low = (kept - high.astype(F32)).astype(BF16)
                total[...] += jnp.dot(high, b, preferred_element_type=F32) + jnp.dot(low, b, preferred_element_type=F32)
            return carry

        lax.fori_loop(0, 8, up, 0)

    def query_part(first, last):
        def query(k, carry):
            rows = pl.ds(pl.multiple_of(k * 512, 512), 512)
            up_q[...] += jnp.dot(hid_all[k], w_q[rows, :], preferred_element_type=F32)
            return carry

        lax.fori_loop(first, last, query, 0)

    w_first(0)
    hid.first_own(0)
    hid.first_own(1)
    hid.second_own(1, 0)
    pack_adapters()
    adapters_send("adp_a", 0)
    l_wq = load(4, q_weight, w_q)
    mark_rows()
    w_spread(0, 0)
    w_spread(0, 1)
    w_second(0)
    attn_own()
    hid.first_fwd(0)
    hid.first_fwd(1)
    hid.second_own(1, 1)
    hid.second_own(1, 2)
    w_spread(0, 2)
    w_first(1)
    loaded(1, l_hid)
    loaded(2, l_attn)
    got("adp_a")
    down_product()
    hid.second_fwd(1, 0)
    w_pass(0, 0)
    w_pass(0, 1)
    attn_fwd()
    w_pass(0, 2)
    w_spread(1, 0)
    w_spread(1, 1)
    w_second(1)
    hid.first_opp(1)
    hid.second_own(1, 3)
    hid.second_fwd(1, 1)
    hid.second_fwd(1, 2)
    w_last(0)
    loaded(3, l_wo)
    w_spread(1, 2)
    w_pass(1, 0)
    w_pass(1, 1)
    hid.second_fwd(1, 3)
    down_across()
    hid.second_own(0, 0)
    hid.second_own(0, 1)
    w_done(0)
    got("attn_opp")
    partial(0)
    send("red0", 1, part.at[0, upper], r_opp.at[0], dev_x[2])
    send("red1", 1, part.at[0, lower], r_opp.at[1], dev_x[1])
    partial(1)
    w_pass(1, 2)
    hid.second_own(0, 2)
    hid.first_opp(0)
    hid.second_own(0, 3)
    w_last(1)
    adapters_send("adp_b", 128)
    down_back()
    w_done(1)
    partial(2)
    send("red2", 1, part.at[1, lower], r_nbr.at[0, lower], dev_x[2])
    send("red3", 1, part.at[2, upper], r_nbr.at[1, upper], dev_x[1])
    hid.second_fwd(0, 0)
    hid.second_fwd(0, 1)
    got("red0")
    part[1, upper, :] = part[1, upper, :] + r_opp[0]
    send("red4", 1, part.at[1, upper], r_nbr.at[0, upper], dev_x[2])
    got("red1")
    part[2, lower, :] = part[2, lower, :] + r_opp[1]
    send("red5", 1, part.at[2, lower], r_nbr.at[1, lower], dev_x[1])
    partial(3)
    hid.second_fwd(0, 2)
    hid.second_fwd(0, 3)
    got("down3")
    got("adp_b")
    up_product()
    part[3] = part[3] + up_o[...]

    for k in (2, 3, 4, 5):
        got(f"red{k}")
    own_cols = pl.ds(pl.multiple_of(t * 512, 512), 512)
    o_blk[...] = (part[3] + r_nbr[0] + r_nbr[1]).astype(BF16)
    out.first_own(0)
    out.first_own(1)
    l_o = load(5, o_blk, a_out.at[:, own_cols])
    hid.last()
    loaded(4, l_wq)
    query_part(0, 8)
    out.second_own(1, 0)
    out.second_own(0, 0)
    for lot in (0, 1, 2):
        gone(lot)
    out.first_fwd(0)
    out.first_fwd(1)
    for i in (1, 2):
        out.second_own(0, i)
        out.second_own(1, i)
    query_part(8, 12)
    out.first_opp(0)
    out.second_own(0, 3)
    out.first_opp(1)
    out.second_own(1, 3)
    out.second_fwd(0, 0)
    out.second_fwd(1, 0)
    out.second_fwd(0, 1)
    out.second_fwd(1, 1)
    query_part(12, 16)
    q_blk[...] = up_q[...].astype(BF16)
    l_q = load(6, q_blk, q_out)
    for i in (2, 3):
        out.second_fwd(0, i)
        out.second_fwd(1, i)
    out.last()
    gone(3)
    loaded(5, l_o)
    loaded(6, l_q)


def body(hidden, attn, q_weight, o_weight, table, adapters, req_slot, req_len, qa, qb, oa, ob):
    hbm = pl.BlockSpec(memory_space=pl.ANY)
    smem = pl.BlockSpec(memory_space=pltpu.SMEM)
    vm = pltpu.VMEM
    qa_t, oa_t = jnp.transpose(qa, (0, 2, 1)), jnp.transpose(oa, (0, 2, 1))
    return pl.pallas_call(
        kernel,
        out_shape=(
            vm((384, 512), BF16),
            vm((384, 8192), BF16),
        ),
        in_specs=[hbm] * 8 + [smem] * 4,
        out_specs=[hbm] * 2,
        scratch_shapes=[
            vm((16, 384, 512), BF16),
            vm((4, 384, 512), BF16),
            vm((4, 4, 512, 512), BF16),
            vm((2, 4, 32, 512), BF16),
            vm((8192, 512), BF16),
            vm((8, 64, 512), BF16),
            vm((8, 64, 512), BF16),
            vm((8, 64, 512), BF16),
            vm((8, 64, 512), BF16),
            vm((8, 256, 512), BF16),
            vm((8, 256, 512), BF16),
            vm((384, 128), jnp.int32),
            vm((384, 128), F32),
            vm((3, 96, 128), F32),
            vm((3, 96, 128), F32),
            vm((2, 96, 128), F32),
            vm((384, 128), F32),
            vm((384, 512), F32),
            vm((384, 512), F32),
            vm((4, 384, 512), F32),
            vm((2, 192, 512), F32),
            vm((2, 384, 512), F32),
            vm((384, 512), BF16),
            vm((384, 512), BF16),
            pltpu.SemaphoreType.DMA((N_SEND,)),
            pltpu.SemaphoreType.DMA((N_RECV,)),
            pltpu.SemaphoreType.DMA((N_LOCAL,)),
        ],
        compiler_params=pltpu.CompilerParams(
            collective_id=0, has_side_effects=True, vmem_limit_bytes=48 * 1024 * 1024
        ),
    )(hidden, attn, q_weight, o_weight, qa_t, qb, oa_t, ob, table, adapters, req_slot, req_len)


def solution(mesh):
    return jax.shard_map(
        body,
        mesh=mesh,
        in_specs=(
            P("group", "tensor"),
            P("group", "tensor"),
            P(None, "tensor"),
            P("tensor", None),
            P(),
            P(),
            P("group", None),
            P("group", None),
            P("group", "tensor", None),
            P("group", None, "tensor"),
            P("group", "tensor", None),
            P("group", None, "tensor"),
        ),
        out_specs=(P("group", "tensor"), P("group", None)),
        check_vma=False,
    )
```

```python
import jax
import jax.numpy as jnp
from jax import lax
from jax.experimental import pallas as pl
from jax.experimental.pallas import tpu as pltpu
from jax.sharding import PartitionSpec as P

MESH = pl.DeviceIdType.MESH
F32 = jnp.float32
BF16 = jnp.bfloat16

N_RECV = 75
N_SEND = 4
N_LOCAL = 11


def mod(a, n):
    return lax.rem(a + n, n)


def kernel(
    hidden, attn, q_weight, o_weight, qa, qb, oa, ob, table_in, adapters_in, req_slot_in, req_len_in,
    q_out, a_out,
    hid_all, attn_all, w_o, w_stage, w_q, qa_v, qb_v, oa_v, ob_v, send_a, recv_a, a_stage,
    owner_v, down_v, down_1, down_2, down_s, down_all, up_q, up_o, part, r_opp, r_nbr, o_blk, q_blk, table, adapters, req_slot, req_len,
    send_sem, recv_sem, local_sem,
):
    g = lax.axis_index("group")
    t = lax.axis_index("tensor")
    z, c = lax.div(g, 2), lax.rem(g, 2)
    y, x = lax.div(t, 4), lax.rem(t, 4)
    ys = [y, mod(y - 1, 4), mod(y + 1, 4), mod(y + 2, 4)]
    xs = [x, mod(x - 1, 4), mod(x + 1, 4), mod(x + 2, 4)]
    gs = [g] + [mod(z + d, 4) * 2 + c for d in (-1, 1, 2)]
    sib = z * 2 + (1 - c)
    gother = [sib] + [mod(z + d, 4) * 2 + (1 - c) for d in (-1, 1)]
    dev_x = [None] + [{"tensor": y * 4 + xs[i]} for i in (1, 2, 3)]
    dev_y = [None] + [{"tensor": ys[i] * 4 + x} for i in (1, 2, 3)]
    dev_z = [None] + [{"group": gs[i]} for i in (1, 2)]
    dev_sib = {"group": sib}

    names, expected, leaving = {}, {}, {}

    def size(ref):
        count = 1
        for extent in ref.shape:
            count *= extent
        return count * ref.dtype.itemsize

    def wait_bytes(sem, count):
        rows = w_q.at[pl.ds(0, count // 1024)]
        pltpu.make_async_copy(rows, rows, sem).wait()

    def send(name, lot, src, dst, dev):
        k = names.setdefault(name, len(names))
        pltpu.make_async_remote_copy(
            src_ref=src, dst_ref=dst, send_sem=send_sem.at[lot], recv_sem=recv_sem.at[k],
            device_id=dev, device_id_type=MESH,
        ).start()
        expected[name] = expected.get(name, 0) + size(src)
        leaving[lot] = leaving.get(lot, 0) + size(src)

    def got(name):
        wait_bytes(recv_sem.at[names[name]], expected.pop(name))

    def gone(lot):
        wait_bytes(send_sem.at[lot], leaving.pop(lot))

    def load(k, src, dst):
        pltpu.make_async_copy(src, dst, local_sem.at[k]).start()
        return size(src)

    def loaded(k, count):
        wait_bytes(local_sem.at[k], count)

    barrier = pltpu.get_barrier_semaphore()
    for i in (1, 2, 3):
        pl.semaphore_signal(barrier, inc=1, device_id=dev_x[i], device_id_type=MESH)
        pl.semaphore_signal(barrier, inc=1, device_id=dev_y[i], device_id_type=MESH)
    for d in range(1, 8):
        pl.semaphore_signal(barrier, inc=1, device_id={"group": mod(g + d, 8)}, device_id_type=MESH)
    tables = [
        pltpu.make_async_copy(src, dst, local_sem.at[7 + i])
        for i, (src, dst) in enumerate(
            ((table_in, table), (adapters_in, adapters), (req_slot_in, req_slot), (req_len_in, req_len))
        )
    ]
    for copy in tables:
        copy.start()
    l_adp = load(0, qa, qa_v) + load(0, oa, oa_v) + load(0, qb, qb_v) + load(0, ob, ob_v)
    l_hid = load(1, hidden, hid_all.at[t])
    l_attn = load(2, attn, attn_all.at[y])
    x_slot = [xs[3], xs[2], xs[1], xs[0]]

    def wcols(i, j):
        return pl.ds(pl.multiple_of(ys[i] * 2048 + x_slot[j] * 512, 512), 512)

    l_wo = sum(load(3, o_weight.at[:, wcols(0, j)], w_o.at[y, j]) for j in range(4))

    def local_index(dest):
        def body(s, found):
            place = table[adapters[dest, s]]
            return jnp.where(lax.div(place, 8) == g, lax.rem(place, 8), found)

        return lax.fori_loop(0, 8, body, jnp.int32(0))

    def pack_adapters():
        for copy in tables:
            copy.wait()
        loaded(0, l_adp)

        def pack(p, carry):
            pair = lax.div(p, 2)
            step = jnp.where(pair == 2, 3, jnp.where(pair == 3, 2, pair))
            core = lax.rem(c + lax.rem(p, 2), 2)
            idx = local_index(mod(z + step, 4) * 2 + core)
            send_a[p, 0:64, :] = qa_v[idx]
            send_a[p, 64:128, :] = oa_v[idx]
            send_a[p, 128:192, :] = qb_v[idx]
            send_a[p, 192:256, :] = ob_v[idx]
            return carry

        lax.fori_loop(0, 8, pack, 0)
        recv_a[g] = send_a[0]

    def mark_rows():
        row = lax.broadcasted_iota(jnp.int32, (384, 128), 0)
        owner_v[...] = jnp.zeros((384, 128), jnp.int32)

        def mark(k, start):
            end = start + req_len[0, k]
            own = lax.div(table[adapters[g, req_slot[0, k]]], 8)
            owner_v[...] = jnp.where((row >= start) & (row < end), own, owner_v[...])
            return end

        lax.fori_loop(0, 16, mark, jnp.int32(0))

    pl.semaphore_wait(barrier, 13)

    class Gather:
        def __init__(self, name, lot, buf, own, cut):
            self.name, self.lot, self.buf, self.own, self.cut = name, lot, buf, own, cut

        def block(self, half, i, j):
            return ys[j] * 4 + xs[i] if half == 0 else ys[i] * 4 + xs[j]

        def devs(self, half):
            return (dev_x, dev_y) if half == 0 else (dev_y, dev_x)

        def rows(self, half, i, j, quarter=None):
            b = self.block(half, i, j)
            start, size = (0, self.cut) if half == 0 else (self.cut, 384 - self.cut)
            if quarter is not None:
                start, size = start + quarter * (size // 2), size // 2
            if len(self.buf.shape) == 3:
                return self.buf.at[b, pl.ds(start, size)]
            return self.buf.at[pl.ds(start, size), pl.ds(pl.multiple_of(b * 512, 512), 512)]

        def src_own(self, half):
            return self.own.at[pl.ds(0, self.cut) if half == 0 else pl.ds(self.cut, 384 - self.cut)]

        def key(self, *what):
            return (self.name,) + what

        def first_own(self, half):
            dev = self.devs(half)[0]
            for to in (2, 1):
                send(self.key(half, "own"), self.lot, self.src_own(half), self.rows(half, 0, 0), dev[to])

        def first_fwd(self, half):
            dev = self.devs(half)[0]
            got(self.key(half, "own"))
            for way in (0, 1):
                ref = self.rows(half, 1 + way, 0, way)
                send(self.key(half, "opp"), self.lot, ref, ref, dev[2 - way])

        def first_opp(self, half):
            got(self.key(half, "opp"))

        def second_own(self, half, i):
            dev = self.devs(half)[1]
            src = self.src_own(half) if i == 0 else self.rows(half, i, 0)
            for to in (2, 1):
                send(self.key(half, i), self.lot, src, self.rows(half, i, 0), dev[to])

        def second_fwd(self, half, i):
            dev = self.devs(half)[1]
            got(self.key(half, i))
            for way in (0, 1):
                ref = self.rows(half, i, 1 + way, way)
                send(self.key("last"), self.lot, ref, ref, dev[2 - way])

        def second_own_cut(self, half, i):
            dev = self.devs(half)[1]
            for piece in (0, 1):
                for way in (0, 1):
                    ref = self.rows(half, i, 0, way ^ piece)
                    send(self.key(half, i, piece), self.lot, ref, ref, dev[2 - way])

        def second_fwd_cut(self, half, i):
            dev = self.devs(half)[1]
            got(self.key(half, i, 0))
            for way in (0, 1):
                ref = self.rows(half, i, 1 + way, way)
                send(self.key("last"), self.lot, ref, ref, dev[2 - way])

        def last_cut(self, half, i):
            got(self.key(half, i, 1))

        def last(self):
            got(self.key("last"))

    hid = Gather("hid", 2, hid_all, hidden, 224)
    out = Gather("out", 3, a_out, o_blk, 192)

    chunks = ((0, 1), (1, 2), (3, 1))

    def wrows(i, ch, grp, half=None):
        if half is None:
            return w_o.at[ys[i], pl.ds(*chunks[ch]), pl.ds(pl.multiple_of(grp * 64, 64), 64)]
        return w_o.at[ys[i], pl.ds(*chunks[ch]), pl.ds(pl.multiple_of(grp * 64 + half * 32, 32), 32)]

    def wrow(i, j, grp):
        return w_o.at[ys[i], j, pl.ds(pl.multiple_of(grp * 64, 64), 64)]

    def w_first(ch):
        for j in range(chunks[ch][0], sum(chunks[ch])):
            for way, to in ((0, 2), (1, 1)):
                rows = pl.ds(pl.multiple_of(g * 64, 64), 64)
                send(("nbr", ch, way), 0, o_weight.at[rows, wcols(to, j)], wrow(0, j, g), dev_y[to])
                rows = pl.ds(pl.multiple_of(g * 64 + way * 32, 32), 32)
                send(("opp", ch), 0, o_weight.at[rows, wcols(3, j)], w_stage.at[way, j], dev_y[to])

    def w_second(ch):
        got(("opp", ch))
        for way in (0, 1):
            send(("opp2", ch), 0, w_stage.at[way, pl.ds(*chunks[ch])], wrows(1 + way, ch, g, way), dev_y[2 - way])

    def w_spread(ch, i):
        got(("nbr", ch, i) if i < 2 else ("opp2", ch))
        ref = wrows(i + 1, ch, g)
        send(("z", ch, i), 0, ref, ref, dev_z[2])
        send(("z", ch, i), 0, ref, ref, dev_z[1])
        send(("sib", ch), 0, ref, ref, dev_sib)

    def w_pass(ch, i):
        got(("z", ch, i))
        for way in (0, 1):
            ref = wrows(i + 1, ch, gs[1 + way], way)
            send(("zopp", ch), 0, ref, ref, dev_z[2 - way])
        for way in (0, 1):
            ref = wrows(i + 1, ch, gs[1 + way])
            send(("sib", ch), 0, ref, ref, dev_sib)

    def w_last(ch):
        got(("zopp", ch))
        for i in range(3):
            ref = wrows(i + 1, ch, gs[3])
            send(("sib", ch), 0, ref, ref, dev_sib)

    def w_done(ch):
        got(("sib", ch))

    def adapters_send(name, first, count):
        rows = pl.ds(first, count)
        for way in (0, 1):
            part_rows = pl.ds(first + count // 2 * way, count // 2)
            send((name, "stage"), 1, send_a.at[pl.ds(6, 2), part_rows], a_stage.at[:, part_rows], dev_z[2 - way])
        for p, to in ((2, gs[2]), (3, gother[2]), (4, gs[1]), (5, gother[1]), (1, sib)):
            send((name, "near"), 1, send_a.at[p, rows], recv_a.at[g, rows], {"group": to})

    def adapters_pass(name, first, count):
        got((name, "stage"))
        for way in (0, 1):
            rows = pl.ds(first + count // 2 * way, count // 2)
            for core, to in ((0, gs[2 - way]), (1, gother[2 - way])):
                send((name, "far"), 1, a_stage.at[core, rows], recv_a.at[gs[1 + way], rows], {"group": to})

    def adapters_got(name):
        got((name, "near"))
        got((name, "far"))

    upper, lower = pl.ds(0, 192), pl.ds(192, 192)

    def attn_own():
        for to in (2, 1):
            send("attn", 2, attn, attn_all.at[y], dev_y[to])

    def attn_fwd():
        got("attn")
        for way, part_rows in ((0, upper), (1, lower)):
            ref = attn_all.at[ys[1 + way], part_rows]
            send("attn_opp", 2, ref, ref, dev_y[2 - way])

    def partial(j):
        def half(h, carry):
            rows = pl.ds(pl.multiple_of(h * 192, 192), 192)
            total = jnp.dot(attn_all[0, rows, :], w_o[0, j], preferred_element_type=F32)
            for i in range(1, 4):
                total = total + jnp.dot(attn_all[i, rows, :], w_o[i, j], preferred_element_type=F32)
            part[j, rows, :] = total
            return carry

        lax.fori_loop(0, 2, half, 0)

    lane = lax.broadcasted_iota(jnp.int32, (384, 128), 1)
    x_off = [mod(x + d, 4) for d in range(4)]

    def piece(v):
        return pl.ds(pl.multiple_of(v * 96, 32), 96)

    def down_product():
        down_v[...] = jnp.zeros((384, 128), F32)

        def down(o, carry):
            a = recv_a[o, 0:128, :]
            from_hid = lax.dot_general(hid_all[t], a, (((1,), (1,)), ((), ())), preferred_element_type=F32)
            from_att = lax.dot_general(attn_all[y], a, (((1,), (1,)), ((), ())), preferred_element_type=F32)
            value = jnp.where(lane < 64, from_hid, from_att)
            down_v[...] = jnp.where(owner_v[...] == o, value, down_v[...])
            return carry

        lax.fori_loop(0, 8, down, 0)
        for d in (1, 2, 3):
            send("down1", 1, down_v.at[piece(x_off[d])], down_1.at[d - 1], {"tensor": y * 4 + x_off[d]})

    def down_across():
        got("down1")
        down_s[0] = down_v[piece(x), :] + down_1[0] + down_1[1] + down_1[2]
        for d in (1, 2, 3):
            send("down2", 1, down_s.at[0], down_2.at[d - 1], {"tensor": mod(y + d, 4) * 4 + x})

    def down_back():
        got("down2")
        down_s[1] = down_s[0] + down_2[0] + down_2[1] + down_2[2]
        for d in (1, 2, 3):
            send("down3", 1, down_s.at[1], down_all.at[piece(x)], {"tensor": y * 4 + x_off[d]})
        down_all[piece(x), :] = down_s[1]

    def up_product(first, total):
        def half(h, carry):
            rows = pl.ds(pl.multiple_of(h * 192, 192), 192)
            value = down_all[rows, :] * 0.5
            high = value.astype(BF16).astype(F32)
            side = lax.broadcasted_iota(jnp.int32, (192, 128), 1) < 64
            left = jnp.where(side == (first == 0), high, pltpu.roll(value - high, 64, 1))
            own = owner_v[rows, :]
            acc = None
            for o in range(8):
                b = recv_a[o, 128 + first : 192 + first, :]
                term = jnp.dot(
                    jnp.where(own == o, left, 0.0).astype(BF16),
                    jnp.concatenate([b, b], axis=0),
                    preferred_element_type=F32,
                )
                acc = term if acc is None else acc + term
            total[rows, :] = acc
            return carry

        lax.fori_loop(0, 2, half, 0)

    def query_part(first, last):
        def query(k, carry):
            rows = pl.ds(pl.multiple_of(k * 512, 512), 512)
            up_q[...] += jnp.dot(hid_all[k], w_q[rows, :], preferred_element_type=F32)
            return carry

        lax.fori_loop(first, last, query, 0)

    w_first(0)
    hid.first_own(0)
    hid.first_own(1)
    hid.second_own(1, 0)
    pack_adapters()
    adapters_send("adp_a", 0, 128)
    l_wq = load(4, q_weight, w_q)
    mark_rows()
    w_spread(0, 0)
    w_spread(0, 1)
    w_first(1)
    w_second(0)
    hid.first_fwd(0)
    adapters_pass("adp_a", 0, 128)
    hid.first_fwd(1)
    hid.second_own(1, 1)
    hid.second_own(1, 2)
    attn_own()
    w_spread(0, 2)
    w_spread(1, 0)
    w_spread(1, 1)
    w_second(1)
    hid.second_fwd(1, 0)
    for i in range(3):
        w_pass(0, i)
    loaded(1, l_hid)
    loaded(2, l_attn)
    adapters_got("adp_a")
    down_product()
    hid.first_opp(1)
    hid.second_own(1, 3)
    hid.second_fwd(1, 1)
    hid.second_fwd(1, 2)
    attn_fwd()
    w_first(2)
    w_pass(1, 0)
    w_pass(1, 1)
    w_spread(1, 2)
    w_last(0)
    down_across()
    hid.second_own(0, 0)
    loaded(3, l_wo)
    w_done(0)
    got("attn_opp")
    partial(0)
    send("red0", 1, part.at[0, upper], r_opp.at[0], dev_x[2])
    send("red1", 1, part.at[0, lower], r_opp.at[1], dev_x[1])
    w_pass(1, 2)
    w_spread(2, 0)
    w_spread(2, 1)
    adapters_send("adp_o", 192, 64)
    w_second(2)
    hid.second_own(0, 1)
    hid.second_fwd(1, 3)
    w_last(1)
    hid.second_own(0, 2)
    hid.first_opp(0)
    hid.second_own(0, 3)
    w_done(1)
    partial(1)
    partial(2)
    down_back()
    send("red3", 1, part.at[2, upper], r_nbr.at[1, upper], dev_x[1])
    w_pass(2, 0)
    w_pass(2, 1)
    got("red0")
    part[1, upper, :] = part[1, upper, :] + r_opp[0]
    send("red4", 1, part.at[1, upper], r_nbr.at[0, upper], dev_x[2])
    send("red2", 1, part.at[1, lower], r_nbr.at[0, lower], dev_x[2])
    got("red1")
    part[2, lower, :] = part[2, lower, :] + r_opp[1]
    send("red5", 1, part.at[2, lower], r_nbr.at[1, lower], dev_x[1])
    w_spread(2, 2)
    hid.second_fwd(0, 0)
    w_pass(2, 2)
    adapters_send("adp_q", 128, 64)
    adapters_pass("adp_o", 192, 64)
    hid.second_fwd(0, 1)
    hid.second_fwd(0, 2)
    w_last(2)
    adapters_pass("adp_q", 128, 64)
    got("down3")
    hid.second_fwd(0, 3)
    w_done(2)
    partial(3)
    adapters_got("adp_o")
    up_product(64, up_o)

    own_cols = pl.ds(pl.multiple_of(t * 512, 512), 512)

    def final(rows):
        o_blk[rows, :] = (part[3, rows, :] + up_o[rows, :] + r_nbr[0, rows, :] + r_nbr[1, rows, :]).astype(BF16)

    got("red3")
    got("red4")
    final(upper)
    out.first_own(0)
    out.second_own(0, 0)
    adapters_got("adp_q")
    up_product(0, up_q)
    got("red2")
    got("red5")
    final(lower)
    out.first_own(1)
    out.second_own(1, 0)
    l_o = load(5, o_blk, a_out.at[:, own_cols])
    for lot in (0, 1, 2):
        gone(lot)
    out.first_fwd(0)
    out.second_own(0, 1)
    out.first_fwd(1)
    out.second_own(1, 1)
    out.second_own(0, 2)
    out.second_own(1, 2)
    hid.last()
    loaded(4, l_wq)
    query_part(0, 8)
    out.second_fwd(0, 0)
    out.first_opp(0)
    out.second_own_cut(0, 3)
    out.second_fwd(1, 0)
    out.first_opp(1)
    out.second_own_cut(1, 3)
    query_part(8, 12)
    out.second_fwd(0, 1)
    out.second_fwd(1, 1)
    query_part(12, 16)
    q_blk[...] = up_q[...].astype(BF16)
    l_q = load(6, q_blk, q_out)
    out.second_fwd(0, 2)
    out.second_fwd(1, 2)
    out.second_fwd_cut(0, 3)
    out.second_fwd_cut(1, 3)
    out.last_cut(0, 3)
    out.last_cut(1, 3)
    out.last()
    gone(3)
    loaded(5, l_o)
    loaded(6, l_q)
    assert len(names) == N_RECV


def store(q_in, a_in, q_out, a_out, sem):
    copies = []
    for i in range(8):
        rows = pl.ds(48 * i, 48)
        copies.append(pltpu.make_async_copy(a_in.at[rows], a_out.at[rows], sem.at[i]))
    copies.append(pltpu.make_async_copy(q_in, q_out, sem.at[8]))
    for copy in copies:
        copy.start()
    for copy in copies:
        copy.wait()


def body(hidden, attn, q_weight, o_weight, table, adapters, req_slot, req_len, qa, qb, oa, ob):
    hbm = pl.BlockSpec(memory_space=pl.ANY)
    vm = pltpu.VMEM
    qa_t, oa_t = jnp.transpose(qa, (0, 2, 1)), jnp.transpose(oa, (0, 2, 1))
    kept = pl.pallas_call(
        kernel,
        out_shape=(
            vm((384, 512), BF16),
            vm((384, 8192), BF16),
        ),
        in_specs=[hbm] * 12,
        out_specs=[hbm] * 2,
        scratch_shapes=[
            vm((16, 384, 512), BF16),
            vm((4, 384, 512), BF16),
            vm((4, 4, 512, 512), BF16),
            vm((2, 4, 32, 512), BF16),
            vm((8192, 512), BF16),
            vm((8, 64, 512), BF16),
            vm((8, 64, 512), BF16),
            vm((8, 64, 512), BF16),
            vm((8, 64, 512), BF16),
            vm((8, 256, 512), BF16),
            vm((8, 256, 512), BF16),
            vm((2, 256, 512), BF16),
            vm((384, 128), jnp.int32),
            vm((384, 128), F32),
            vm((3, 96, 128), F32),
            vm((3, 96, 128), F32),
            vm((2, 96, 128), F32),
            vm((384, 128), F32),
            vm((384, 512), F32),
            vm((384, 512), F32),
            vm((4, 384, 512), F32),
            vm((2, 192, 512), F32),
            vm((2, 384, 512), F32),
            vm((384, 512), BF16),
            vm((384, 512), BF16),
            pltpu.SMEM((64,), jnp.int32),
            pltpu.SMEM((8, 8), jnp.int32),
            pltpu.SMEM((1, 16), jnp.int32),
            pltpu.SMEM((1, 16), jnp.int32),
            pltpu.SemaphoreType.DMA((N_SEND,)),
            pltpu.SemaphoreType.DMA((N_RECV,)),
            pltpu.SemaphoreType.DMA((N_LOCAL,)),
        ],
        compiler_params=pltpu.CompilerParams(
            collective_id=0, has_side_effects=True, vmem_limit_bytes=48 * 1024 * 1024
        ),
    )(hidden, attn, q_weight, o_weight, qa_t, qb, oa_t, ob, table, adapters, req_slot, req_len)
    return pl.pallas_call(
        store,
        out_shape=(jax.ShapeDtypeStruct((384, 512), BF16), jax.ShapeDtypeStruct((384, 8192), BF16)),
        in_specs=[hbm] * 2,
        out_specs=[hbm] * 2,
        scratch_shapes=[pltpu.SemaphoreType.DMA((9,))],
        compiler_params=pltpu.CompilerParams(vmem_limit_bytes=1024 * 1024),
    )(*kept)


def solution(mesh):
    return jax.shard_map(
        body,
        mesh=mesh,
        in_specs=(
            P("group", "tensor"),
            P("group", "tensor"),
            P(None, "tensor"),
            P("tensor", None),
            P(),
            P(),
            P("group", None),
            P("group", None),
            P("group", "tensor", None),
            P("group", None, "tensor"),
            P("group", "tensor", None),
            P("group", None, "tensor"),
        ),
        out_specs=(P("group", "tensor"), P("group", None)),
        check_vma=False,
    )
```
